32 devices in a mesh: groups: 2 (over x), ctx: 16 (over z, y, core).
Axes of the slice: x: 2, y: 2, z: 4, core: 2. Of those that a mesh axis runs over, the one named last changes fastest.
Arguments:
- hidden: bfloat16 [256, 8192], P('groups', 'ctx'), parts along dimension 0, may hold values from -6 to 6
- attn_gain: bfloat16 [8192], P('ctx'), may hold values from 0.25 to 1.75
- q_weight: bfloat16 [8192, 8192], P(None, 'ctx'), may hold values from -0.0625 to 0.0625
- q_gain: bfloat16 [128], replicated, may hold values from 0.25 to 1.75
- key_cache: bfloat16 [49152, 1024], P(('groups', 'ctx')), parts along dimension 0, may hold values from -64 to 64
- value_cache: bfloat16 [49152, 1024], P(('groups', 'ctx')), parts along dimension 0, may hold values from -6 to 6
- block_limit: int32 [256], P('groups'), parts along dimension 0, may hold values from 0 to 191, as said below
- out_weight: bfloat16 [8192, 8192], P('ctx'), may hold values from -0.09375 to 0.09375
- next_gain: bfloat16 [8192], P('ctx'), may hold values from 0.25 to 1.75
- next_weight: bfloat16 [8192, 8192], P(None, 'ctx'), may hold values from -0.0625 to 0.0625
Outputs:
- new_hidden: bfloat16 [256, 8192], P('groups', 'ctx'), parts along dimension 0
- next_queries: bfloat16 [256, 8192], P('groups', 'ctx'), parts along dimension 0
The draws below stay inside these ranges and needn't reach their ends.
There are 2 independent parts, one for each index of `groups`. The reference program is written for one: setup_inputs(seed, part) draws one part's arguments, and reference() takes and returns one part's arrays. A program takes and returns all parts, laid end to end along the dimension named above; an argument that names none is the same for every part. Nothing has to cross between parts.
Inputs may be any that keep to these rules, and one draw needn't show every extreme that they name: Text token i may attend the visual blocks 0 to block_limit[i], each of 128 visual tokens; some token reaches the last block and some only the first.
All inputs are finite; a program needn't handle non-finite values.
Results may differ from the reference program's by a relative error of at most 0.015.
Values may be sent and summed in bfloat16 or wider, within the bound.
A program may use at most 64 MiB of HBM per device.

```python
import jax
import jax.numpy as jnp
from jax import lax

D = 8192
HEADS = 64
KV_HEADS = 8
HEAD_DIM = 128
QUERIES = 128
BLK = 128
V_TOTAL = 24576
BLOCKS = 192


def draw_key_cache(key, part):
    first_key = jax.random.fold_in(jax.random.fold_in(key, 11), 0)
    shape = (V_TOTAL, KV_HEADS * HEAD_DIM)
    base = 3.0 * jax.random.truncated_normal(first_key, -6.0, 6.0, shape, jnp.float32)
    return base.astype(jnp.bfloat16)


def draw_block_limit(key, part):
    first_key, second_key, third_key = jax.random.split(jax.random.fold_in(key, 23), 3)
    limits = jax.random.randint(first_key, (QUERIES,), 0, BLOCKS)
    highest = jax.random.randint(second_key, (), 0, QUERIES)
    lowest = (highest + 1 + jax.random.randint(third_key, (), 0, QUERIES - 1)) % QUERIES
    limits = limits.at[highest].set(BLOCKS - 1).at[lowest].set(0)
    return limits.astype(jnp.int32)


def spiked(array, rng, source, target, shards_of, factor):
    def block_of(axis_at):
        return (jnp.arange(array.shape[axis_at]) // (array.shape[axis_at] // shards_of)).reshape((-1,) + (1,) * (array.ndim - 1 - axis_at))

    one_side = jax.random.permutation(rng, shards_of)[block_of(target)]
    far = (block_of(target) + shards_of // 2) % shards_of
    return jnp.where((block_of(source) == one_side) | (block_of(source) == far), factor * array, array)


def levels(key, extent, shards, low, top_value):
    loudness = 1.0
    for dim, blocks in shards:
        steps = jax.random.uniform(jax.random.fold_in(jax.random.fold_in(key, 6), dim), (blocks,), jnp.float32, low / len(shards), top_value / len(shards))
        loudness = loudness * jnp.repeat(jnp.exp(steps), extent[dim] // blocks).reshape((-1,) + (1,) * (len(extent) - 1 - dim))
    return loudness


def noise(stream_key, dims, scale, most, cuts=(), kind=jnp.bfloat16):
    values = jax.random.normal(stream_key, dims, jnp.float32) * scale
    if len(cuts) > 0:
        values = levels(stream_key, dims, cuts, -0.22, 0.18) * values
    return jnp.clip(values, min=-most, max=most).astype(kind)


def gaussian_with(key, extent, width, bound, pieces, heavy, held_as=jnp.bfloat16):
    entries = width * jax.random.normal(key, extent, jnp.float32)
    if pieces:
        entries = entries * levels(key, extent, pieces, -0.22, 0.18)
    return jnp.clip(spiked(entries, jax.random.fold_in(key, 3), *heavy), -bound, bound).astype(held_as)


def setup_inputs(seed: int = 0, part: int = 0) -> dict:
    seeds = jax.random.split(jax.random.key(seed), 11)
    part_splits = jax.random.split(jax.random.fold_in(seeds[10], part), 11)
    hidden = noise(part_splits[0], (QUERIES, D), 1.0, 6.0, ((1, 16),))
    attn_gain = jnp.clip(1.0 + 0.15 * jax.random.normal(seeds[1], (D,), jnp.float32), 0.25, 1.75).astype(jnp.bfloat16)
    q_weight = noise(seeds[2], (D, HEADS * HEAD_DIM), D ** -0.5, 0.0625, ((1, 16),))
    q_gain = jnp.clip(1.0 + 0.15 * jax.random.normal(seeds[3], (HEAD_DIM,), jnp.float32), 0.25, 1.75).astype(jnp.bfloat16)
    key_cache = draw_key_cache(jax.random.fold_in(jax.random.fold_in(seeds[10], part), 71), part)
    value_cache = noise(part_splits[5], (V_TOTAL, KV_HEADS * HEAD_DIM), 1.0, 6.0, ((0, 16),))
    block_limit = draw_block_limit(jax.random.fold_in(jax.random.fold_in(seeds[10], part), 71), part)
    out_weight = gaussian_with(seeds[7], (HEADS * HEAD_DIM, D), (HEADS * HEAD_DIM) ** -0.5, 0.09375, ((0, 16),), (0, 1, 16, 2.0))
    next_gain = jnp.clip(1.0 + 0.15 * jax.random.normal(seeds[8], (D,), jnp.float32), 0.25, 1.75).astype(jnp.bfloat16)
    next_weight = noise(seeds[9], (D, HEADS * HEAD_DIM), D ** -0.5, 0.0625, ((1, 16),))
    return {"hidden": hidden, "attn_gain": attn_gain, "q_weight": q_weight, "q_gain": q_gain, "key_cache": key_cache, "value_cache": value_cache, "block_limit": block_limit, "out_weight": out_weight, "next_gain": next_gain, "next_weight": next_weight}


def rms_rows(rows_in, gain):
    values = rows_in.astype(jnp.float32)
    square_mean = lax.optimization_barrier(jnp.mean(values * values, axis=-1, keepdims=True))
    return (values * lax.rsqrt(square_mean + 1e-05) * gain.astype(jnp.float32)).astype(jnp.bfloat16)

def reference(hidden, attn_gain, q_weight, q_gain, key_cache, value_cache, block_limit, out_weight, next_gain, next_weight):
    normed = rms_rows(hidden, attn_gain)
    query = jnp.dot(normed, q_weight, preferred_element_type=jnp.float32)
    query = query.reshape(QUERIES, HEADS, HEAD_DIM)
    head_mean = lax.optimization_barrier(jnp.mean(query * query, axis=-1, keepdims=True))
    query_normed = (query * lax.rsqrt(head_mean + 1e-05) * q_gain.astype(jnp.float32)).astype(jnp.bfloat16)
    positions = jnp.arange(V_TOTAL, dtype=jnp.int32) // BLK
    allowed = positions[None, :] <= block_limit[:, None]
    scale = HEAD_DIM ** (-0.5)
    per_group = HEADS // KV_HEADS

    def one_head(head):
        group = (head // per_group).astype(jnp.int32)
        keys = lax.dynamic_slice_in_dim(key_cache, group * HEAD_DIM, HEAD_DIM, 1)
        values = lax.dynamic_slice_in_dim(value_cache, group * HEAD_DIM, HEAD_DIM, 1)
        single = lax.dynamic_index_in_dim(query_normed, head, 1, keepdims=False)
        scores = jnp.dot(single, keys.T, preferred_element_type=jnp.float32) * scale
        scores = jnp.where(allowed, scores, -jnp.inf)
        top = lax.optimization_barrier(jnp.max(scores, axis=-1, keepdims=True))
        expo = jnp.exp(scores - top)
        denominator = lax.optimization_barrier(jnp.sum(expo, axis=-1, keepdims=True))
        summed = jnp.dot(expo.astype(jnp.bfloat16), values, preferred_element_type=jnp.float32)
        return (summed / denominator).astype(jnp.bfloat16)
    attended = lax.map(one_head, jnp.arange(HEADS, dtype=jnp.int32))
    attended = jnp.transpose(attended, (1, 0, 2)).reshape(QUERIES, HEADS * HEAD_DIM)
    mixed = jnp.dot(attended, out_weight, preferred_element_type=jnp.float32)
    new_hidden = (hidden.astype(jnp.float32) + mixed).astype(jnp.bfloat16)
    renormed = rms_rows(new_hidden, next_gain)
    next_queries = jnp.dot(renormed, next_weight, preferred_element_type=jnp.float32).astype(jnp.bfloat16)
    return (new_hidden, next_queries)
```

```python
import jax
import jax.numpy as jnp
from jax import lax
from jax.sharding import PartitionSpec as P

BLK = 128


EPSILON = 1e-05


def normalize_project(share, gain_share, weight):
    whole, gains = (
        lax.all_gather(share, "ctx", axis=1, tiled=True),
        lax.all_gather(gain_share, "ctx", axis=0, tiled=True),
    )
    values = whole.astype(jnp.float32)
    factor = lax.rsqrt(jnp.mean(values * values, axis=1, keepdims=True) + EPSILON)
    normed = (values * factor * gains.astype(jnp.float32)).astype(jnp.bfloat16)
    return jnp.dot(normed, weight, preferred_element_type=jnp.float32)


def on_device(
    hidden,
    attn_gain,
    q_weight,
    q_gain,
    key_cache,
    value_cache,
    block_limit,
    out_weight,
    next_gain,
    next_weight,
):
    queries = hidden.shape[0]
    head_dim = q_gain.shape[0]
    devices = lax.axis_size("ctx")
    query = normalize_project(hidden, attn_gain, q_weight)
    heads_here = query.shape[1] // head_dim
    heads_total = heads_here * devices
    kv_heads = key_cache.shape[1] // head_dim
    group_size = heads_total // kv_heads
    shaped = query.reshape(queries, heads_here, head_dim)
    head_mean = jnp.mean(shaped * shaped, axis=-1, keepdims=True)
    query_normed = (shaped * lax.rsqrt(head_mean + EPSILON) * q_gain.astype(jnp.float32)).astype(
        jnp.bfloat16
    )
    local_tokens = key_cache.shape[0]
    device = lax.axis_index("ctx")
    blocks_here = (device * local_tokens + jnp.arange(local_tokens, dtype=jnp.int32)) // BLK
    allowed = blocks_here[None, :] <= block_limit[:, None]
    scale = head_dim ** (-0.5)
    stacked = jnp.swapaxes(query_normed, 0, 1)
    gathered = lax.all_gather(stacked, "ctx", axis=0, tiled=True)
    gathered = gathered.reshape(kv_heads, group_size * queries, head_dim)
    mask = jnp.tile(allowed, (group_size, 1))

    def one_group(group):
        keys = lax.dynamic_slice_in_dim(key_cache, group * head_dim, head_dim, 1)
        values = lax.dynamic_slice_in_dim(value_cache, group * head_dim, head_dim, 1)
        rows = lax.dynamic_index_in_dim(gathered, group, 0, keepdims=False)
        scores = lax.dot_general(
            rows, keys, (((1,), (1,)), ((), ())), preferred_element_type=jnp.float32
        )
        scores = jnp.where(mask, scores * scale, -jnp.inf)
        top = jnp.maximum(jnp.max(scores, axis=1), -1e30)
        expo = jnp.exp(scores - top[:, None])
        sums = jnp.dot(expo.astype(jnp.bfloat16), values, preferred_element_type=jnp.float32)
        return sums, top, jnp.sum(expo, axis=1)

    sums, top, total = lax.map(one_group, jnp.arange(kv_heads, dtype=jnp.int32))
    decay = jnp.exp(top - lax.pmax(top, "ctx"))
    sums = (sums * decay[:, :, None]).astype(jnp.bfloat16).reshape(heads_total, queries, head_dim)
    total = (total * decay).reshape(heads_total, queries)
    sums = lax.psum_scatter(sums, "ctx", scatter_dimension=0, tiled=True)
    total = lax.psum_scatter(total, "ctx", scatter_dimension=0, tiled=True)
    attended = (sums.astype(jnp.float32) / total[:, :, None]).astype(jnp.bfloat16)
    attended = jnp.swapaxes(attended, 0, 1).reshape(queries, heads_here * head_dim)
    mixed = lax.psum_scatter(
        lax.dot_general(
            out_weight, attended, (((0,), (1,)), ((), ())), preferred_element_type=jnp.float32
        ),
        "ctx",
        scatter_dimension=0,
        tiled=True,
    )
    new_hidden = (hidden.astype(jnp.float32) + mixed.T).astype(jnp.bfloat16)
    next_queries = normalize_project(new_hidden, next_gain, next_weight).astype(jnp.bfloat16)
    return (new_hidden, next_queries)


def solution(mesh):
    in_specs = (
        P("groups", "ctx"),
        P("ctx"),
        P(None, "ctx"),
        P(),
        P(("groups", "ctx"), None),
        P(("groups", "ctx"), None),
        P("groups"),
        P("ctx", None),
        P("ctx"),
        P(None, "ctx"),
    )
    out_specs = (P("groups", "ctx"), P("groups", "ctx"))
    return jax.shard_map(
        on_device, mesh=mesh, in_specs=in_specs, out_specs=out_specs, check_vma=False
    )
```

```python
import functools
import math

import jax
import jax.numpy as jnp
from jax import lax
from jax.experimental import pallas as pl
from jax.experimental.pallas import tpu as pltpu
from jax.sharding import PartitionSpec as P

BLK = 128
EPSILON = 1e-05
MESH = pl.DeviceIdType.MESH
BF16, F32 = jnp.bfloat16, jnp.float32


def loop(count, body):
    def step(i, carry):
        body(i)
        return carry

    lax.fori_loop(0, count, step, 0)


def kernel(
    n,
    group_size,
    block_in,
    q_gain_ref,
    limit_ref,
    qw_hbm,
    key_hbm,
    value_hbm,
    ow_hbm,
    nw_hbm,
    hidden_out,
    next_out,
    qw,
    keys,
    values,
    ow,
    nw,
    first,
    queries_all,
    second,
    sums,
    stats,
    mixed,
    sums_core,
    stats_core,
    mixed_core,
    sums_y,
    stats_y,
    mixed_y,
    sums_up,
    stats_up,
    mixed_up,
    sums_down,
    stats_down,
    mixed_down,
    acc,
    squares,
    limits,
    attended,
    sems,
    local_sems,
):
    depth = n // 4
    me = lax.axis_index("ctx")
    core, y, z = lax.rem(me, 2), lax.rem(me // 2, 2), me // 4
    rows, width = hidden_out.shape
    features = n * width
    head_dim = q_gain_ref.shape[1]
    heads = width // head_dim
    tokens = keys.shape[0]

    def at(zz, yy, cc):
        return zz * 4 + yy * 2 + cc

    other_core, other_y = at(z, y, 1 - core), at(z, 1 - y, core)
    above, below = at(z + 1, y, core), at(z - 1, y, core)

    loads = [
        pltpu.make_async_copy(src, dst, local_sems.at[i])
        for i, (src, dst) in enumerate(
            [
                (block_in, first.at[me]),
                (qw_hbm, qw),
                (key_hbm, keys),
                (value_hbm, values),
                (ow_hbm, ow),
                (nw_hbm, nw),
            ]
        )
    ]
    for load in loads:
        load.start()

    barrier = pltpu.get_barrier_semaphore()

    def greet(device):
        pl.semaphore_signal(barrier, inc=1, device_id={"ctx": device}, device_id_type=MESH)

    greet(other_core)
    greet(other_y)
    pl.when(z + 1 < depth)(lambda: greet(above))
    pl.when(z > 0)(lambda: greet(below))
    peers = 2 + jnp.where(z + 1 < depth, 1, 0) + jnp.where(z > 0, 1, 0)
    pl.semaphore_wait(barrier, peers)

    for head in range(heads):
        limits[head * rows : (head + 1) * rows, :] = jnp.broadcast_to(limit_ref[...], (rows, BLK))

    def remote(src, dst, send, recv, device):
        return pltpu.make_async_remote_copy(
            src_ref=src,
            dst_ref=dst,
            send_sem=sems.at[send],
            recv_sem=sems.at[recv],
            device_id={"ctx": device},
            device_id_type=MESH,
        )

    used = [0]
    drains = []

    def gather(buffer):
        base = used[0]
        used[0] += n + 5 * depth
        send = base + n

        def copy(block, device, sem):
            return remote(buffer.at[block], buffer.at[block], sem, base + block, device)

        def to_above(zz):
            return copy(at(zz, y, core), above, send + zz)

        def to_below(zz):
            return copy(at(zz, y, core), below, send + depth + zz)

        def to_y(zz):
            return copy(at(zz, y, core), other_y, send + 2 * depth + zz)

        def to_core(zz, yy):
            return copy(at(zz, yy, core), other_core, send + 3 * depth + 2 * zz + yy)

        def arrive(block):
            copy(block, other_core, send).wait_recv()

        def column(step, sign):
            zz = z + sign * step

            @pl.when((zz >= 0) & (zz < depth))
            def _():
                if step > 0:
                    arrive(at(zz, y, core))
                if step == 0 or sign < 0:
                    pl.when(z + 1 < depth)(lambda: to_above(zz).start())
                if step == 0 or sign > 0:
                    pl.when(z > 0)(lambda: to_below(zz).start())
                to_y(zz).start()
                to_core(zz, y).start()

        def beside(step, sign):
            zz = z + sign * step

            @pl.when((zz >= 0) & (zz < depth))
            def _():
                arrive(at(zz, 1 - y, core))
                to_core(zz, 1 - y).start()

        for step in range(depth + 1):
            if step < depth:
                for sign in (-1, 1) if step else (-1,):
                    column(step, sign)
            if step > 0:
                for sign in (-1, 1) if step > 1 else (-1,):
                    beside(step - 1, sign)

        def drain():
            def one(zz):
                pl.when((zz <= z) & (z + 1 < depth))(lambda: to_above(zz).wait_send())
                pl.when((zz >= z) & (z > 0))(lambda: to_below(zz).wait_send())
                to_y(zz).wait_send()
                to_core(zz, 0).wait_send()
                to_core(zz, 1).wait_send()

            loop(depth, one)

        drains.append(drain)
        return arrive

    def reduce(arrays, compute, combine):
        starts = []
        for _ in arrays:
            starts.append(used[0])
            used[0] += 10 * depth

        def copies(kind, zz, yy=0):
            made = []
            for base, (part, from_core, from_y, from_below, from_above) in zip(starts, arrays):
                if kind == 0:
                    slot, room, where = 2 * zz + yy, 2 * depth, 0
                    src, dst, device = part.at[at(zz, yy, 1 - core)], from_core, other_core
                elif kind == 1:
                    slot, room, where = zz, depth, 4 * depth
                    src, dst, device = part.at[at(zz, 1 - y, core)], from_y, other_y
                elif kind == 2:
                    slot, room, where = zz, depth, 6 * depth
                    src, dst, device = part.at[at(zz, y, core)], from_below, above
                else:
                    slot, room, where = zz, depth, 8 * depth
                    src, dst, device = part.at[at(zz, y, core)], from_above, below
                sem = base + where + slot
                made.append(remote(src, dst.at[slot], sem, sem + room, device))
            return made

        def begin(*which):
            for copy in copies(*which):
                copy.start()

        def received(*which):
            for copy in copies(*which):
                copy.wait_recv()

        def sent(*which):
            for copy in copies(*which):
                copy.wait_send()

        def add(block, which, slot):
            combine(block, [array[which].at[slot] for array in arrays])

        def send_core(i):
            zz, yy = lax.rem(i, depth), jnp.where(i < depth, 1 - y, y)
            compute(at(zz, yy, 1 - core))
            begin(0, zz, yy)

        def send_y(zz):
            block = at(zz, 1 - y, core)
            compute(block)
            received(0, zz, 1 - y)
            add(block, 1, 2 * zz + 1 - y)
            begin(1, zz)

        def keep(zz):
            block = at(zz, y, core)
            compute(block)
            received(0, zz, y)
            add(block, 1, 2 * zz + y)
            received(1, zz)
            add(block, 2, zz)

        loop(2 * depth, send_core)
        loop(depth, send_y)
        loop(depth, keep)

        def along(k):
            high, low = depth - 1 - k, k

            @pl.when(high > z)
            def _():
                @pl.when(z > 0)
                def _():
                    received(2, high)
                    add(at(high, y, core), 3, high)

                begin(2, high)

            @pl.when(low < z)
            def _():
                @pl.when(z + 1 < depth)
                def _():
                    received(3, low)
                    add(at(low, y, core), 4, low)

                begin(3, low)

        loop(depth, along)

        @pl.when(z > 0)
        def _():
            received(2, z)
            add(me, 3, z)

        @pl.when(z + 1 < depth)
        def _():
            received(3, z)
            add(me, 4, z)

        def drain():
            def one(zz):
                sent(0, zz, 0)
                sent(0, zz, 1)
                sent(1, zz)
                pl.when(zz > z)(lambda: sent(2, zz))
                pl.when(zz < z)(lambda: sent(3, zz))

            loop(depth, one)

        drains.append(drain)

    def project(buffer, gain_row, weight, arrive):
        acc[...] = jnp.zeros_like(acc)
        squares[...] = jnp.zeros_like(squares)

        def term(block):
            part = buffer[block, :rows, :].astype(F32)
            gain = first[block, rows : rows + 16, :].astype(F32)[gain_row : gain_row + 1, :]
            squared = part * part
            total = squared[:, :BLK]
            for start in range(BLK, width, BLK):
                total += squared[:, start : start + BLK]
            squares[...] += total
            depth_rows = pl.ds(pl.multiple_of(block * width, width), width)
            acc[...] += jnp.dot(
                (part * gain).astype(BF16), weight[depth_rows, :], preferred_element_type=F32
            )

        loop(n // 2, lambda i: term(2 * i + core))

        def last(i):
            block = 2 * i + 1 - core
            arrive(block)
            term(block)

        loop(n // 2, last)
        mean = jnp.sum(squares[...], axis=1, keepdims=True) * (1.0 / features)
        return acc[...] * lax.rsqrt(mean + EPSILON)

    loads[0].wait()
    arrive = gather(first)
    loads[1].wait()
    query = project(first, 0, qw, arrive)
    for head in range(heads):
        one = query[:, head * head_dim : (head + 1) * head_dim]
        mean = jnp.mean(one * one, axis=1, keepdims=True)
        queries_all[me, head * rows : (head + 1) * rows, :] = (
            one * lax.rsqrt(mean + EPSILON) * q_gain_ref[...].astype(F32)
        ).astype(BF16)

    arrive = gather(queries_all)
    loop(n // 2, lambda i: arrive(2 * i + 1 - core))
    loads[2].wait()
    loads[3].wait()

    factor = head_dim**-0.5 * math.log2(math.e)
    first_block = me * (tokens // BLK)
    chunk = min(2 * rows, heads * rows)

    def attend(block):
        group = (block * heads) // group_size
        columns = pl.ds(pl.multiple_of(group * head_dim, head_dim), head_dim)
        for start in range(0, heads * rows, chunk):
            query_rows = queries_all[block, start : start + chunk, :]
            scores = lax.dot_general(
                query_rows, keys[:, columns], (((1,), (1,)), ((), ())), preferred_element_type=F32
            )
            limit = limits[start : start + chunk, :]
            tiles = [
                jnp.where(
                    limit >= first_block + j, scores[:, j * BLK : (j + 1) * BLK] * factor, -jnp.inf
                )
                for j in range(tokens // BLK)
            ]
            top = functools.reduce(jnp.maximum, tiles)
            top = jnp.maximum(jnp.max(top, axis=1, keepdims=True), -1e30)
            tiles = [jnp.exp2(tile - top) for tile in tiles]
            total = jnp.sum(functools.reduce(jnp.add, tiles), axis=1, keepdims=True)
            weights = jnp.concatenate([tile.astype(BF16) for tile in tiles], axis=1)
            summed = jnp.dot(weights, values[:, columns], preferred_element_type=F32)
            sums[block, start : start + chunk, :] = summed.astype(BF16)
            for inner in range(0, chunk, rows):
                head = (start + inner) // rows
                for row, value in ((head, top), (heads + head, total)):
                    spread = jnp.broadcast_to(value[inner : inner + rows, :], (rows, rows))
                    stats[block, row : row + 1, :] = spread.T[:1, :]

    def merge(block, arrived):
        more_sums, more_stats = arrived
        mine, theirs = stats[block], more_stats[...]
        top = jnp.maximum(mine[:heads], theirs[:heads])
        decay, decay_more = jnp.exp2(mine[:heads] - top), jnp.exp2(theirs[:heads] - top)
        stats[block, :heads, :] = top
        stats[block, heads : 2 * heads, :] = (
            mine[heads : 2 * heads] * decay + theirs[heads : 2 * heads] * decay_more
        )
        for head in range(heads):
            span = slice(head * rows, (head + 1) * rows)
            one = jnp.broadcast_to(decay[head : head + 1, :], (rows, rows)).T
            two = jnp.broadcast_to(decay_more[head : head + 1, :], (rows, rows)).T
            sums[block, span, :] = (
                sums[block, span, :].astype(F32) * one[:, :1]
                + more_sums[span, :].astype(F32) * two[:, :1]
            ).astype(BF16)

    reduce(
        [
            (sums, sums_core, sums_y, sums_up, sums_down),
            (stats, stats_core, stats_y, stats_up, stats_down),
        ],
        attend,
        merge,
    )
    for head in range(heads):
        total = jnp.broadcast_to(stats[me, heads + head : heads + head + 1, :], (rows, rows)).T
        attended[:, head * head_dim : (head + 1) * head_dim] = (
            sums[me, head * rows : (head + 1) * rows, :].astype(F32) / total[:, :1]
        ).astype(BF16)
    loads[4].wait()

    def mix(block):
        columns = pl.ds(pl.multiple_of(block * width, width), width)
        mixed[block] = jnp.dot(
            attended[...], ow[:, columns], preferred_element_type=F32
        ).astype(BF16)

    def total_of(block, arrived):
        mixed[block] = (mixed[block].astype(F32) + arrived[0][...].astype(F32)).astype(BF16)

    reduce([(mixed, mixed_core, mixed_y, mixed_up, mixed_down)], mix, total_of)
    fresh = (first[me, :rows, :].astype(F32) + mixed[me].astype(F32)).astype(BF16)
    hidden_out[...] = fresh
    second[me] = fresh
    arrive = gather(second)
    loads[5].wait()
    next_out[...] = project(second, 1, nw, arrive).astype(BF16)
    for drain in drains:
        drain()


def on_device(
    hidden,
    attn_gain,
    q_weight,
    q_gain,
    key_cache,
    value_cache,
    block_limit,
    out_weight,
    next_gain,
    next_weight,
):
    n = lax.axis_size("ctx")
    depth = n // 4
    rows, width = hidden.shape
    head_dim = q_gain.shape[0]
    heads = width // head_dim
    group_size = heads * n // (key_cache.shape[1] // head_dim)
    block = jnp.concatenate(
        [hidden, attn_gain[None], next_gain[None], jnp.zeros((14, width), hidden.dtype)], axis=0
    )
    tall, lines = heads * rows, max(8, 2 * heads)

    def slots(count):
        return [
            pltpu.VMEM((count, tall, head_dim), BF16),
            pltpu.VMEM((count, lines, rows), F32),
            pltpu.VMEM((count, rows, width), BF16),
        ]

    vmem, hbm = pl.BlockSpec(memory_space=pltpu.VMEM), pl.BlockSpec(memory_space=pl.ANY)
    return pl.pallas_call(
        functools.partial(kernel, n, group_size),
        out_shape=[jax.ShapeDtypeStruct((rows, width), BF16)] * 2,
        in_specs=[vmem] * 3 + [hbm] * 5,
        out_specs=[vmem] * 2,
        scratch_shapes=[
            pltpu.VMEM(q_weight.shape, BF16),
            pltpu.VMEM(key_cache.shape, BF16),
            pltpu.VMEM(value_cache.shape, BF16),
            pltpu.VMEM(out_weight.shape, BF16),
            pltpu.VMEM(next_weight.shape, BF16),
            pltpu.VMEM((n, rows + 16, width), BF16),
            pltpu.VMEM((n, tall, head_dim), BF16),
            pltpu.VMEM((n, rows, width), BF16),
            *slots(n),
            *slots(2 * depth),
            *slots(depth),
            *slots(depth),
            *slots(depth),
            pltpu.VMEM((rows, width), F32),
            pltpu.VMEM((rows, BLK), F32),
            pltpu.VMEM((tall, BLK), jnp.int32),
            pltpu.VMEM((rows, width), BF16),
            pltpu.SemaphoreType.DMA((3 * (n + 5 * depth) + 30 * depth,)),
            pltpu.SemaphoreType.DMA((6,)),
        ],
        compiler_params=pltpu.CompilerParams(
            collective_id=0, has_side_effects=True, vmem_limit_bytes=67043328
        ),
    )(
        block,
        q_gain[None],
        block_limit[:, None],
        q_weight,
        key_cache,
        value_cache,
        out_weight,
        next_weight,
    )


def solution(mesh):
    in_specs = (
        P("groups", "ctx"),
        P("ctx"),
        P(None, "ctx"),
        P(),
        P(("groups", "ctx"), None),
        P(("groups", "ctx"), None),
        P("groups"),
        P("ctx", None),
        P("ctx"),
        P(None, "ctx"),
    )
    out_specs = (P("groups", "ctx"), P("groups", "ctx"))

    def step(*args):
        return tuple(on_device(*args))

    return jax.shard_map(step, mesh=mesh, in_specs=in_specs, out_specs=out_specs, check_vma=False)
```

```python
import functools
import math

import jax
import jax.numpy as jnp
from jax import lax
from jax.experimental import pallas as pl
from jax.experimental.pallas import tpu as pltpu
from jax.sharding import PartitionSpec as P

BLK = 128
EPSILON = 1e-05
MESH = pl.DeviceIdType.MESH
BF16, F32 = jnp.bfloat16, jnp.float32


def loop(count, body):
    def step(i, carry):
        body(i)
        return carry

    lax.fori_loop(0, count, step, 0)


def kernel(
    n,
    group_size,
    hidden_in,
    attn_gain_ref,
    next_gain_ref,
    q_gain_ref,
    limit_ref,
    qw_hbm,
    key_hbm,
    value_hbm,
    ow_hbm,
    nw_hbm,
    hidden_out,
    next_out,
    qw,
    keys,
    values,
    ow,
    nw,
    first,
    queries_all,
    second,
    sums,
    stats,
    mixed,
    sums_core,
    stats_core,
    mixed_core,
    sums_y,
    stats_y,
    mixed_y,
    sums_up,
    stats_up,
    mixed_up,
    sums_down,
    stats_down,
    mixed_down,
    acc,
    squares,
    limits,
    attended,
    sems,
    local_sems,
):
    depth = n // 4
    me = lax.axis_index("ctx")
    core, y, z = lax.rem(me, 2), lax.rem(me // 2, 2), me // 4
    rows, width = hidden_out.shape
    features = n * width
    head_dim = q_gain_ref.shape[1]
    heads = width // head_dim
    tokens = keys.shape[0]

    def at(zz, yy, cc):
        return zz * 4 + yy * 2 + cc

    other_core, other_y = at(z, y, 1 - core), at(z, 1 - y, core)
    above, below = at(z + 1, y, core), at(z - 1, y, core)

    loads = [
        pltpu.make_async_copy(src, dst, local_sems.at[i])
        for i, (src, dst) in enumerate(
            [
                (hidden_in, first.at[me, pl.ds(0, rows)]),
                (qw_hbm, qw),
                (key_hbm, keys),
                (value_hbm, values),
                (ow_hbm, ow),
                (nw_hbm, nw),
            ]
        )
    ]
    for load in loads:
        load.start()

    line = lax.broadcasted_iota(jnp.int32, (16, width), 0)
    gains = [jnp.broadcast_to(g[...].astype(F32), (16, width)) for g in (attn_gain_ref, next_gain_ref)]
    first[me, rows : rows + 16, :] = jnp.where(line == 0, gains[0], gains[1]).astype(BF16)

    barrier = pltpu.get_barrier_semaphore()

    def greet(device):
        pl.semaphore_signal(barrier, inc=1, device_id={"ctx": device}, device_id_type=MESH)

    greet(other_core)
    greet(other_y)
    pl.when(z + 1 < depth)(lambda: greet(above))
    pl.when(z > 0)(lambda: greet(below))
    peers = 2 + jnp.where(z + 1 < depth, 1, 0) + jnp.where(z > 0, 1, 0)
    pl.semaphore_wait(barrier, peers)

    limit_rows = jnp.broadcast_to(limit_ref[...], (rows, rows)).T[:, :1]
    for head in range(heads):
        limits[head * rows : (head + 1) * rows, :] = jnp.broadcast_to(limit_rows, (rows, BLK))

    before, after = z, depth - 1 - z
    lone, paired = jnp.abs(after - before), jnp.minimum(after, before)

    def farthest(i):
        j = jnp.maximum(i - lone, 0)
        distance = paired - lax.div(j, 2)
        near = z + jnp.where(lax.rem(j, 2) == 0, distance, -distance)
        return jnp.where(i < lone, jnp.where(after > before, depth - 1 - i, i), near)

    def remote(src, dst, send, recv, device):
        return pltpu.make_async_remote_copy(
            src_ref=src,
            dst_ref=dst,
            send_sem=sems.at[send],
            recv_sem=sems.at[recv],
            device_id={"ctx": device},
            device_id_type=MESH,
        )

    used = [0]
    drains = []

    def gather(buffer, ready, consume):
        base = used[0]
        used[0] += n + 5 * depth
        send = base + n

        def copy(block, device, sem):
            return remote(buffer.at[block], buffer.at[block], sem, base + block, device)

        def to_above(zz):
            return copy(at(zz, y, core), above, send + zz)

        def to_below(zz):
            return copy(at(zz, y, core), below, send + depth + zz)

        def to_y(zz):
            return copy(at(zz, y, core), other_y, send + 2 * depth + zz)

        def to_core(zz, yy):
            return copy(at(zz, yy, core), other_core, send + 3 * depth + 2 * zz + yy)

        def arrive(block):
            copy(block, other_core, send).wait_recv()

        def column(step, sign):
            zz = z + sign * step
            start = step == 0
            fresh = jnp.logical_not(start) if sign > 0 else step >= 0

            @pl.when((zz >= 0) & (zz < depth) & fresh)
            def _():
                pl.when(step > 0)(lambda: arrive(at(zz, y, core)))
                if sign < 0:
                    pl.when(z + 1 < depth)(lambda: to_above(zz).start())
                    pl.when(start & (z > 0))(lambda: to_below(zz).start())
                else:
                    pl.when(z > 0)(lambda: to_below(zz).start())
                to_y(zz).start()
                to_core(zz, y).start()

        def beside(step, sign):
            zz = z + sign * step

            @pl.when((zz >= 0) & (zz < depth) & (step >= (1 if sign > 0 else 0)))
            def _():
                arrive(at(zz, 1 - y, core))
                to_core(zz, 1 - y).start()

        def turn(step):
            column(step, -1)
            column(step, 1)
            beside(step - 1, -1)
            beside(step - 1, 1)
            pl.when(step == 1)(ready)

            def use(i):
                distance = step - 1
                upward = i >= 2
                zz = z + jnp.where(upward, distance, -distance)
                fresh = (distance > 0) | jnp.logical_not(upward)

                @pl.when((distance >= 0) & (zz >= 0) & (zz < depth) & fresh)
                def _():
                    consume(at(zz, lax.rem(i, 2), core))

            loop(4, use)

        loop(depth + 1, turn)

        def drain():
            def one(zz):
                pl.when((zz <= z) & (z + 1 < depth))(lambda: to_above(zz).wait_send())
                pl.when((zz >= z) & (z > 0))(lambda: to_below(zz).wait_send())
                to_y(zz).wait_send()
                to_core(zz, 0).wait_send()
                to_core(zz, 1).wait_send()

            loop(depth, one)

        drains.append(drain)
        return arrive

    def reduce(arrays, compute_other, compute, combine):
        starts = []
        for _ in arrays:
            starts.append(used[0])
            used[0] += 10 * depth

        def copies(kind, zz, yy=0):
            made = []
            for base, (part, from_core, from_y, from_below, from_above) in zip(starts, arrays):
                if kind == 0:
                    slot, room, where = 2 * zz + yy, 2 * depth, 0
                    src, dst, device = part.at[at(zz, yy, 1 - core)], from_core, other_core
                elif kind == 1:
                    slot, room, where = zz, depth, 4 * depth
                    src, dst, device = part.at[at(zz, 1 - y, core)], from_y, other_y
                elif kind == 2:
                    slot, room, where = zz, depth, 6 * depth
                    src, dst, device = part.at[at(zz, y, core)], from_below, above
                else:
                    slot, room, where = zz, depth, 8 * depth
                    src, dst, device = part.at[at(zz, y, core)], from_above, below
                sem = base + where + slot
                made.append(remote(src, dst.at[slot], sem, sem + room, device))
            return made

        def begin(*which):
            for copy in copies(*which):
                copy.start()

        def received(*which):
            for copy in copies(*which):
                copy.wait_recv()

        def sent(*which):
            for copy in copies(*which):
                copy.wait_send()

        def add(block, which, slot):
            combine(block, [array[which].at[slot] for array in arrays])

        def spread(zz):
            def across(i):
                yy = jnp.where(i == 0, 1 - y, y)
                compute_other(at(zz, yy, 1 - core))
                begin(0, zz, yy)

            def here(i):
                yy = jnp.where(i == 0, 1 - y, y)
                block = at(zz, yy, core)
                compute(block)
                received(0, zz, yy)
                add(block, 1, 2 * zz + yy)
                pl.when(i == 0)(lambda: begin(1, zz))

            loop(2, across)
            loop(2, here)

        def along(zz):
            block = at(zz, y, core)
            received(1, zz)
            add(block, 2, zz)

            @pl.when(zz > z)
            def _():
                @pl.when(z > 0)
                def _():
                    received(2, zz)
                    add(block, 3, zz)

                begin(2, zz)

            @pl.when(zz < z)
            def _():
                @pl.when(z + 1 < depth)
                def _():
                    received(3, zz)
                    add(block, 4, zz)

                begin(3, zz)

        def step(i):
            pl.when(i < depth)(lambda: spread(farthest(i)))
            pl.when(i > 0)(lambda: along(farthest(i - 1)))

        loop(depth + 1, step)

        @pl.when(z > 0)
        def _():
            received(2, z)
            add(me, 3, z)

        @pl.when(z + 1 < depth)
        def _():
            received(3, z)
            add(me, 4, z)

        def drain():
            def one(zz):
                sent(0, zz, 0)
                sent(0, zz, 1)
                sent(1, zz)
                pl.when(zz > z)(lambda: sent(2, zz))
                pl.when(zz < z)(lambda: sent(3, zz))

            loop(depth, one)

        drains.append(drain)

    def project(buffer, gain_row, weight, load):
        acc[...] = jnp.zeros_like(acc)
        squares[...] = jnp.zeros_like(squares)

        def term(block):
            part = buffer[block, :rows, :].astype(F32)
            gain = first[block, rows : rows + 16, :].astype(F32)[gain_row : gain_row + 1, :]
            squared = part * part
            total = squared[:, :BLK]
            for start in range(BLK, width, BLK):
                total += squared[:, start : start + BLK]
            squares[...] += total
            depth_rows = pl.ds(pl.multiple_of(block * width, width), width)
            acc[...] += jnp.dot(
                (part * gain).astype(BF16), weight[depth_rows, :], preferred_element_type=F32
            )

        arrive = gather(buffer, load.wait, term)

        def last(i):
            block = 2 * i + 1 - core
            arrive(block)
            term(block)

        loop(n // 2, last)
        mean = jnp.sum(squares[...], axis=1, keepdims=True) * (1.0 / features)
        return acc[...] * lax.rsqrt(mean + EPSILON)

    loads[0].wait()
    query = project(first, 0, qw, loads[1])
    for head in range(heads):
        one = query[:, head * head_dim : (head + 1) * head_dim]
        mean = jnp.mean(one * one, axis=1, keepdims=True)
        queries_all[me, head * rows : (head + 1) * rows, :] = (
            one * lax.rsqrt(mean + EPSILON) * q_gain_ref[...].astype(F32)
        ).astype(BF16)

    factor = head_dim**-0.5 * math.log2(math.e)
    first_block = me * (tokens // BLK)
    chunk = min(2 * rows, heads * rows)

    def attend(block):
        group = (block * heads) // group_size
        columns = pl.ds(pl.multiple_of(group * head_dim, head_dim), head_dim)
        for start in range(0, heads * rows, chunk):
            query_rows = queries_all[block, start : start + chunk, :]
            scores = lax.dot_general(
                query_rows, keys[:, columns], (((1,), (1,)), ((), ())), preferred_element_type=F32
            )
            limit = limits[start : start + chunk, :]
            tiles = [
                jnp.where(
                    limit >= first_block + j, scores[:, j * BLK : (j + 1) * BLK] * factor, -jnp.inf
                )
                for j in range(tokens // BLK)
            ]
            top = functools.reduce(jnp.maximum, tiles)
            top = jnp.maximum(jnp.max(top, axis=1, keepdims=True), -1e30)
            tiles = [jnp.exp2(tile - top) for tile in tiles]
            total = jnp.sum(functools.reduce(jnp.add, tiles), axis=1, keepdims=True)
            weights = jnp.concatenate([tile.astype(BF16) for tile in tiles], axis=1)
            summed = jnp.dot(weights, values[:, columns], preferred_element_type=F32)
            sums[block, start : start + chunk, :] = summed.astype(BF16)
            for inner in range(0, chunk, rows):
                head = (start + inner) // rows
                for row, value in ((head, top), (heads + head, total)):
                    spread = jnp.broadcast_to(value[inner : inner + rows, :], (rows, rows))
                    stats[block, row : row + 1, :] = spread.T[:1, :]

    def merge(block, arrived):
        more_sums, more_stats = arrived
        mine, theirs = stats[block], more_stats[...]
        top = jnp.maximum(mine[:heads], theirs[:heads])
        decay, decay_more = jnp.exp2(mine[:heads] - top), jnp.exp2(theirs[:heads] - top)
        stats[block, :heads, :] = top
        stats[block, heads : 2 * heads, :] = (
            mine[heads : 2 * heads] * decay + theirs[heads : 2 * heads] * decay_more
        )
        for head in range(heads):
            span = slice(head * rows, (head + 1) * rows)
            one = jnp.broadcast_to(decay[head : head + 1, :], (rows, rows)).T
            two = jnp.broadcast_to(decay_more[head : head + 1, :], (rows, rows)).T
            sums[block, span, :] = (
                sums[block, span, :].astype(F32) * one[:, :1]
                + more_sums[span, :].astype(F32) * two[:, :1]
            ).astype(BF16)

    def caches_ready():
        loads[2].wait()
        loads[3].wait()

    arrive = gather(queries_all, caches_ready, attend)

    def attend_late(block):
        arrive(block)
        attend(block)

    reduce(
        [
            (sums, sums_core, sums_y, sums_up, sums_down),
            (stats, stats_core, stats_y, stats_up, stats_down),
        ],
        attend_late,
        lambda block: None,
        merge,
    )
    for head in range(heads):
        total = jnp.broadcast_to(stats[me, heads + head : heads + head + 1, :], (rows, rows)).T
        attended[:, head * head_dim : (head + 1) * head_dim] = (
            sums[me, head * rows : (head + 1) * rows, :].astype(F32) / total[:, :1]
        ).astype(BF16)
    loads[4].wait()

    def mix(block):
        columns = pl.ds(pl.multiple_of(block * width, width), width)
        mixed[block] = jnp.dot(
            attended[...], ow[:, columns], preferred_element_type=F32
        ).astype(BF16)

    def total_of(block, arrived):
        mixed[block] = (mixed[block].astype(F32) + arrived[0][...].astype(F32)).astype(BF16)

    reduce([(mixed, mixed_core, mixed_y, mixed_up, mixed_down)], mix, mix, total_of)
    fresh = (first[me, :rows, :].astype(F32) + mixed[me].astype(F32)).astype(BF16)
    hidden_out[...] = fresh
    second[me] = fresh
    next_out[...] = project(second, 1, nw, loads[5]).astype(BF16)
    for drain in drains:
        drain()


def on_device(
    hidden,
    attn_gain,
    q_weight,
    q_gain,
    key_cache,
    value_cache,
    block_limit,
    out_weight,
    next_gain,
    next_weight,
):
    n = lax.axis_size("ctx")
    depth = n // 4
    rows, width = hidden.shape
    head_dim = q_gain.shape[0]
    heads = width // head_dim
    group_size = heads * n // (key_cache.shape[1] // head_dim)
    tall, lines = heads * rows, max(8, 2 * heads)

    def slots(count):
        return [
            pltpu.VMEM((count, tall, head_dim), BF16),
            pltpu.VMEM((count, lines, rows), F32),
            pltpu.VMEM((count, rows, width), BF16),
        ]

    vmem, hbm = pl.BlockSpec(memory_space=pltpu.VMEM), pl.BlockSpec(memory_space=pl.ANY)
    return pl.pallas_call(
        functools.partial(kernel, n, group_size),
        out_shape=[jax.ShapeDtypeStruct((rows, width), BF16)] * 2,
        in_specs=[vmem] * 5 + [hbm] * 5,
        out_specs=[vmem] * 2,
        scratch_shapes=[
            pltpu.VMEM(q_weight.shape, BF16),
            pltpu.VMEM(key_cache.shape, BF16),
            pltpu.VMEM(value_cache.shape, BF16),
            pltpu.VMEM(out_weight.shape, BF16),
            pltpu.VMEM(next_weight.shape, BF16),
            pltpu.VMEM((n, rows + 16, width), BF16),
            pltpu.VMEM((n, tall, head_dim), BF16),
            pltpu.VMEM((n, rows, width), BF16),
            *slots(n),
            *slots(2 * depth),
            *slots(depth),
            *slots(depth),
            *slots(depth),
            pltpu.VMEM((rows, width), F32),
            pltpu.VMEM((rows, BLK), F32),
            pltpu.VMEM((tall, BLK), jnp.int32),
            pltpu.VMEM((rows, width), BF16),
            pltpu.SemaphoreType.DMA((3 * (n + 5 * depth) + 30 * depth,)),
            pltpu.SemaphoreType.DMA((6,)),
        ],
        compiler_params=pltpu.CompilerParams(
            collective_id=0, has_side_effects=True, vmem_limit_bytes=67043328
        ),
    )(
        hidden,
        attn_gain[None],
        next_gain[None],
        q_gain[None],
        block_limit[None],
        q_weight,
        key_cache,
        value_cache,
        out_weight,
        next_weight,
    )


def solution(mesh):
    in_specs = (
        P("groups", "ctx"),
        P("ctx"),
        P(None, "ctx"),
        P(),
        P(("groups", "ctx"), None),
        P(("groups", "ctx"), None),
        P("groups"),
        P("ctx", None),
        P("ctx"),
        P(None, "ctx"),
    )
    out_specs = (P("groups", "ctx"), P("groups", "ctx"))

    def step(*args):
        return tuple(on_device(*args))

    return jax.shard_map(step, mesh=mesh, in_specs=in_specs, out_specs=out_specs, check_vma=False)
```
